128 devices in a mesh: prod: 32 (over x, y, core), pre: 4 (over z).
Axes of the slice: x: 4, y: 4, z: 4, core: 2. Of those that a mesh axis runs over, the one named last changes fastest.
Arguments:
- potentials: bfloat16 [512, 16, 512], P(('prod', 'pre')), may hold values from -6 to 6
- injected: float32 [512, 16, 512], P(('prod', 'pre')), may hold values from -6 to 6
- near_blocks: bfloat16 [512, 4, 512, 512], P('prod', 'pre'), may hold values from -0.125 to 0.125
- near_cols: int32 [512, 4], P('prod', 'pre'), may hold values from 0 to 511, as said below
- row_basis: bfloat16 [512, 16, 512], P('prod'), may hold values from -1.5 to 1.5
- col_basis: bfloat16 [512, 16, 512], P(('prod', 'pre')), may hold values from -0.25 to 0.25
- basis_ranks: int32 [512], P(('prod', 'pre')), may hold values from 1 to 16
- couplings: bfloat16 [512, 16, 8192], P('prod', None, 'pre'), may hold values from -0.0625 to 0.0625
- inverses: bfloat16 [512, 512, 512], P(('prod', 'pre')), may hold values from -0.25 to 0.25
Outputs:
- residual: float32 [512, 16, 512], P(('prod', 'pre'))
- corrected: float32 [512, 16, 512], P(('prod', 'pre'))
The draws below stay inside these ranges and needn't reach their ends.
Inputs may be any that keep to these rules, and one draw needn't show every extreme that they name: near_cols[i, 0] = i; near_cols[i, 1] is i + 8 or i - 8; every other entry differs from i by 1 to 7.
All inputs are finite; a program needn't handle non-finite values.
Results may differ from the reference program's by a relative error of at most 0.012.
Values may be sent and summed in bfloat16 or wider, within the bound.
No kernel may reach another device: no remote copies, remote signals or barrier semaphores. Data moves between devices by JAX's collectives and lax.ppermute only.
A program may use at most 64 MiB of HBM per device.

```python
import jax
import jax.numpy as jnp
from jax import lax

P_SIZE = 512
K = 16
S = 16
NC = 512
CPD = 4
BAND = 8
NB = 4
N_PROD = 32
N_PRE = 4


def draw_near_cols(key, part):
    first_key, second_key = jax.random.split(key)
    row_ids = jnp.arange(NC, dtype=jnp.int32)
    signs = jax.random.randint(first_key, (NC,), 0, 2).astype(jnp.int32) * 2 - 1
    steps_up = jnp.arange(1, BAND, dtype=jnp.int32)
    candidates = jnp.concatenate([steps_up, -steps_up])
    row_keys = jax.random.split(second_key, NC)
    shuffled = jax.vmap(lambda one_key: jax.random.permutation(one_key, candidates))(row_keys)[:, :NB - 2]
    offsets = jnp.concatenate([jnp.zeros((NC, 1), jnp.int32), (signs * BAND)[:, None], shuffled.astype(jnp.int32)], axis=1)
    columns = row_ids[:, None] + offsets
    outside = (columns < 0) | (columns >= NC)
    return jnp.where(outside, row_ids[:, None] - offsets, columns).astype(jnp.int32)


def touch_ends(values, stream_key, smallest, high):
    shape = values.shape
    spot = [jax.random.randint(jax.random.fold_in(stream_key, axis), (), 0, shape[axis]) for axis in range(len(shape))]
    values = values.at[tuple(spot)].set(smallest)
    longest = shape.index(max(shape))
    spot[longest] = (spot[longest] + 1) % shape[longest]
    return values.at[tuple(spot)].set(high)


def level_of(stream_key, shape, shards, smallest, high):
    loudness, own = 1.0, jax.random.fold_in(stream_key, 6)
    for position, parts in shards:
        steps = jnp.exp(jax.random.uniform(jax.random.fold_in(own, position), (parts,), jnp.float32, smallest / len(shards), high / len(shards)))
        loudness = loudness * jnp.repeat(steps, shape[position] // parts).reshape([-1 if axis == position else 1 for axis in range(len(shape))])
    return loudness


def centred(stream_key, dims, scale, most, pieces=(), kind=jnp.bfloat16):
    array = jax.random.normal(stream_key, dims, jnp.float32) * scale
    if len(pieces) > 0:
        array = level_of(stream_key, dims, pieces, -0.22, 0.18) * array
    return jnp.clip(array, min=-most, max=most).astype(kind)


def setup_inputs(seed: int = 0) -> dict:
    keys = jax.random.split(jax.random.key(seed), 10)
    potentials = centred(keys[0], (NC, S, P_SIZE), 1.0, 6.0, ((0, 128),))
    injected = centred(keys[1], (NC, S, P_SIZE), 1.0, 6.0, ((0, 128),), jnp.float32)
    near_blocks = centred(keys[2], (NC, NB, P_SIZE, P_SIZE), (NB * P_SIZE) ** -0.5, 0.125, ((0, 32), (1, 4)))
    near_cols = draw_near_cols(jax.random.fold_in(keys[9], 71), 0)
    row_basis = centred(keys[4], (NC, K, P_SIZE), K ** -0.5, 1.5, ((0, 32),))
    col_basis = centred(keys[5], (NC, K, P_SIZE), P_SIZE ** -0.5, 0.25, ((0, 128),))
    basis_ranks = touch_ends(jax.random.randint(keys[6], (NC,), 1, K + 1), jax.random.fold_in(keys[6], 1), 1, K).astype(jnp.int32)
    couplings = centred(keys[7], (NC, K, NC * K), (NC * K) ** -0.5, 0.0625, ((0, 32), (2, 4)))
    inverses = centred(keys[8], (NC, P_SIZE, P_SIZE), P_SIZE ** -0.5, 0.25, ((0, 128),))
    return {"potentials": potentials, "injected": injected, "near_blocks": near_blocks, "near_cols": near_cols, "row_basis": row_basis, "col_basis": col_basis, "basis_ranks": basis_ranks, "couplings": couplings, "inverses": inverses}


def reference(potentials, injected, near_blocks, near_cols, row_basis, col_basis, basis_ranks, couplings, inverses):
    coeffs = lax.dot_general(potentials, col_basis, (((2,), (2,)), ((0,), (0,))), preferred_element_type=jnp.float32)
    levels = jnp.arange(K, dtype=jnp.int32)[None, :]
    kept_levels = levels < basis_ranks[:, None]
    coeffs = jnp.where(kept_levels[:, None, :], coeffs, jnp.zeros_like(coeffs)).astype(jnp.bfloat16)
    ordered = coeffs.reshape(N_PROD, N_PRE, CPD, S, K).transpose(1, 0, 2, 4, 3).reshape(NC * K, S)
    weights = jnp.dot(couplings.reshape(NC * K, NC * K), ordered, preferred_element_type=jnp.float32)
    weights = weights.reshape(NC, K, S).astype(jnp.bfloat16)
    far_field = lax.dot_general(weights, row_basis, (((1,), (1,)), ((0,), (0,))), preferred_element_type=jnp.float32)

    def near_row(block_pair):
        blocks, columns = block_pair
        picked = potentials[columns]
        return lax.dot_general(picked, blocks, (((0, 2), (0, 2)), ((), ())), preferred_element_type=jnp.float32)

    near_field = lax.map(near_row, (near_blocks, near_cols))
    residual = injected - (near_field + far_field)
    halfway = residual.astype(jnp.bfloat16)
    corrected = lax.dot_general(halfway, inverses, (((2,), (2,)), ((0,), (0,))), preferred_element_type=jnp.float32)
    return residual, corrected
```

```python
import functools

import jax
import jax.numpy as jnp
from jax import lax
from jax.experimental import pallas as pl
from jax.experimental.pallas import tpu as pltpu
from jax.sharding import PartitionSpec as P

AXES = ("prod", "pre")
GRAY = (0, 1, 3, 2)
NT = (((1,), (1,)), ((), ()))
F32 = jnp.float32
BF16 = jnp.bfloat16


def pairs(rule):
    table = []
    for p in range(32):
        for a in range(4):
            q, b = rule(p, a)
            table.append((p * 4 + a, q * 4 + b))
    return table


def first_mask(p):
    return 1 if p % 2 == 0 else 3


CORE_SWAP = pairs(lambda p, a: (p ^ 1, a))
Y_SWAPS = tuple(pairs(lambda p, a, m=m: (p ^ (2 * m), a)) for m in (1, 3))
X_SWAPS = tuple(pairs(lambda p, a, m=m: (p ^ (8 * m), a)) for m in (1, 3))
Z_FIRST = pairs(lambda p, a: (p, a ^ first_mask(p)))
Z_SECOND = pairs(lambda p, a: (p, a ^ first_mask(p) ^ 2))
OTHER_CHIP = pairs(lambda p, a: ((p + 1) % 32 if p % 2 else (p - 1) % 32, a))


def send(x, table):
    return lax.ppermute(x, AXES, table)


def place():
    p = lax.axis_index("prod")
    a = lax.axis_index("pre")
    core = p & 1
    first = 1 + 2 * core
    second = 3 - 2 * core
    return p, a, core, first, second


def coeff_kernel(pot_ref, basis_ref, ranks_ref, out_ref):
    p = lax.axis_index("prod")
    pot = pot_ref[...].reshape(64, 512)
    basis = basis_ref[...].reshape(64, 512)
    both = jnp.concatenate([basis, basis], axis=0)
    full = lax.dot_general(pot, both, NT, preferred_element_type=F32)
    lane = lax.broadcasted_iota(jnp.int32, (16, 128), 1)
    here = (lane >> 6) == (p & 1)
    total = jnp.zeros((16, 128), F32)
    for j in range(4):
        keep = here & (((lane >> 4) & 3) == j) & ((lane & 15) < ranks_ref[j])
        total = total + jnp.where(keep, full[j * 16:(j + 1) * 16, :], 0.0)
    out_ref[...] = total.astype(BF16)


def far_kernel(near_half_ref, far_half_ref, couplings_ref, row_ref, out_ref, gathered):
    p = lax.axis_index("prod")
    x = p >> 3
    y = (p >> 1) & 3
    for r in range(16):
        chip = (x ^ GRAY[r // 4]) * 4 + (y ^ GRAY[r % 4])
        piece = near_half_ref[r] if r < 8 else far_half_ref[r - 8]
        gathered[:, pl.ds(pl.multiple_of(chip * 128, 128), 128)] = piece
    weights = lax.dot_general(gathered[...], couplings_ref[...], NT, preferred_element_type=F32)
    tall = jnp.concatenate([weights] * 16, axis=0)
    row = lax.broadcasted_iota(jnp.int32, (256, 256), 0) >> 4
    col = lax.broadcasted_iota(jnp.int32, (256, 256), 1) >> 4
    spread = jnp.where(row == col, tall, 0.0).astype(BF16)
    out_ref[...] = jnp.dot(spread, row_ref[...], preferred_element_type=F32)


def select_kernel(own_ref, other_ref, group_ref, chip_ref, out_ref):
    p, a, core, first, second = place()
    for z in range(4):
        d = a ^ z
        slot = jnp.where(d == 0, 0, jnp.where(d == first, 1, jnp.where(d == second, 2, 3)))
        at = pl.multiple_of((slot & 1) * 4, 4)
        piece = jnp.where(slot < 2, own_ref[pl.ds(at, 4)], other_ref[pl.ds(at, 4)])
        group_ref[z * 4:(z + 1) * 4] = piece
        to_chip = (z < 2) == (core == 1) if False else ((z >> 1) ^ core) == 1

        @pl.when(to_chip)
        def _():
            chip_ref[(z & 1) * 4:(z & 1) * 4 + 4] = piece

        @pl.when(jnp.logical_not(to_chip))
        def _():
            out_ref[(z & 1) * 4:(z & 1) * 4 + 4] = piece


def near_kernel(keep, cols_ref, group_ref, chip_ref, outer_ref, near_ref, far_ref, out_ref):
    p, a, core, first, second = place()
    base = p * 16
    for half in range(2):
        if keep:
            piece = a if half == 0 else a ^ second
        else:
            piece = a ^ first if half == 0 else a ^ 2
        for j in range(4):
            i = piece * 4 + j
            c = cols_ref[i] - base
            below = c < 0
            above = c >= 16
            halo = jnp.clip(jnp.where(below, c + 8, c - 16), 0, 7)
            from_chip = (below & (core == 1)) | (above & (core == 0))
            inside = jnp.logical_not(below | above)
            picked = jnp.where(from_chip, chip_ref[halo], outer_ref[halo])
            picked = jnp.where(inside, group_ref[jnp.clip(c, 0, 15)], picked)
            block = lax.dot_general(picked, near_ref[i], NT, preferred_element_type=F32)
            rows = pl.ds(pl.multiple_of(i * 16, 16), 16)
            out_ref[half * 4 + j] = (block + far_ref[rows, :]).astype(out_ref.dtype)


def fold_kernel(kept_ref, got_ref, out_ref):
    out_ref[...] = (kept_ref[4:8] + got_ref[4:8].astype(F32)).astype(BF16)


def final_kernel(kept_ref, got_ref, last_ref, injected_ref, inverse_ref, residual_ref, corrected_ref):
    for j in range(4):
        total = kept_ref[j] + got_ref[j].astype(F32) + last_ref[j].astype(F32)
        residual = injected_ref[j] - total
        residual_ref[j] = residual
        corrected_ref[j] = lax.dot_general(
            residual.astype(BF16), inverse_ref[j], NT, preferred_element_type=F32
        )


VMEM = pl.BlockSpec(memory_space=pltpu.VMEM)
SMEM = pl.BlockSpec(memory_space=pltpu.SMEM)


def call(kernel, out_shape, in_specs, name, scratch=(), flops=0, moved=0):
    many = isinstance(out_shape, (list, tuple))
    return pl.pallas_call(
        kernel,
        out_shape=out_shape,
        in_specs=in_specs,
        out_specs=[VMEM] * len(out_shape) if many else VMEM,
        scratch_shapes=list(scratch),
        compiler_params=pltpu.CompilerParams(vmem_limit_bytes=24 * 2**20),
        cost_estimate=pl.CostEstimate(flops=flops, bytes_accessed=moved, transcendentals=0),
        name=name,
    )


def shape(dims, dtype):
    return jax.ShapeDtypeStruct(dims, dtype)


def local(
    potentials,
    injected,
    near_blocks,
    near_cols,
    row_basis,
    col_basis,
    basis_ranks,
    couplings,
    inverses,
):
    first_z = send(potentials, Z_FIRST)
    coeffs = call(coeff_kernel, shape((16, 128), BF16), [VMEM, VMEM, SMEM], "coeffs", moved=2**17)(
        potentials, col_basis, basis_ranks
    )
    gathered = (coeffs + send(coeffs, CORE_SWAP))[None]
    for table in (Y_SWAPS[0], Y_SWAPS[1], X_SWAPS[0]):
        gathered = jnp.concatenate([gathered, send(gathered, table)], axis=0)
    others = send(gathered, X_SWAPS[1])
    own_pair = jnp.concatenate([potentials, first_z], axis=0)
    second_z = send(own_pair, Z_SECOND)
    group, to_chip, to_outer = call(
        select_kernel,
        [shape((16, 16, 512), BF16), shape((8, 16, 512), BF16), shape((8, 16, 512), BF16)],
        [VMEM, VMEM], "select", moved=2**19,
    )(own_pair, second_z)
    outer = send(to_outer, OTHER_CHIP)
    chip = send(to_chip, CORE_SWAP)
    far = call(
        far_kernel, shape((256, 512), F32), [VMEM] * 4, "far",
        scratch=[pltpu.VMEM((16, 2048), BF16)], moved=2**21, flops=2**26,
    )(gathered, others, couplings.reshape(256, 2048), row_basis.reshape(256, 512))
    blocks = near_blocks.reshape(16, 512, 512)
    cols = near_cols.reshape(16)
    near_specs = [SMEM] + [VMEM] * 5
    sent = call(
        functools.partial(near_kernel, False), shape((8, 16, 512), BF16), near_specs, "near_sent",
        moved=2**22, flops=2**26,
    )(cols, group, chip, outer, blocks, far)
    got = send(sent, Z_FIRST)
    kept = call(
        functools.partial(near_kernel, True), shape((8, 16, 512), F32), near_specs, "near_kept",
        moved=2**22, flops=2**26,
    )(cols, group, chip, outer, blocks, far)
    folded = call(fold_kernel, shape((4, 16, 512), BF16), [VMEM] * 2, "fold", moved=2**18)(kept, got)
    last = send(folded, Z_SECOND)
    return call(
        final_kernel, [shape((4, 16, 512), F32), shape((4, 16, 512), F32)], [VMEM] * 5, "final",
        moved=2**21, flops=2**25,
    )(kept, got, last, injected, inverses)


def solution(mesh):
    return jax.shard_map(
        local,
        mesh=mesh,
        in_specs=(
            P(("prod", "pre"), None, None),
            P(("prod", "pre"), None, None),
            P("prod", "pre", None, None),
            P("prod", "pre"),
            P("prod", None, None),
            P(("prod", "pre"), None, None),
            P(("prod", "pre")),
            P("prod", None, "pre"),
            P(("prod", "pre"), None, None),
        ),
        out_specs=(P(("prod", "pre"), None, None), P(("prod", "pre"), None, None)),
        check_vma=False,
    )
```

```python
import functools

import jax
import jax.numpy as jnp
from jax import lax
from jax.experimental import pallas as pl
from jax.experimental.pallas import tpu as pltpu
from jax.sharding import PartitionSpec as P


AXES = ("prod", "pre")
GRAY = (0, 1, 3, 2)
NT = (((1,), (1,)), ((), ()))
F32 = jnp.float32
BF16 = jnp.bfloat16


def pairs(rule):
    table = []
    for p in range(32):
        for a in range(4):
            q, b = rule(p, a)
            table.append((p * 4 + a, q * 4 + b))
    return table


def first_mask(p):
    return 1 if p % 2 == 0 else 3


CORE_SWAP = pairs(lambda p, a: (p ^ 1, a))
Y_SWAPS = tuple(pairs(lambda p, a, m=m: (p ^ (2 * m), a)) for m in (1, 3))
X_SWAPS = tuple(pairs(lambda p, a, m=m: (p ^ (8 * m), a)) for m in (1, 3))
Z_FIRST = pairs(lambda p, a: (p, a ^ first_mask(p)))
Z_SECOND = pairs(lambda p, a: (p, a ^ first_mask(p) ^ 2))
OTHER_CHIP = pairs(lambda p, a: (p, a ^ 1) if p in (0, 31) else (p + 1 if p % 2 else p - 1, a))


def send(x, table):
    return lax.ppermute(x, AXES, table)


def place():
    p = lax.axis_index("prod")
    a = lax.axis_index("pre")
    core = p & 1
    first = 1 + 2 * core
    second = 3 - 2 * core
    return p, a, core, first, second


def coeff_kernel(pot_hbm, basis_hbm, ranks_hbm, out_ref, room_ref, pot_ref, basis_ref, ranks_ref, sems):
    p = lax.axis_index("prod")
    copies = [
        pltpu.make_async_copy(pot_hbm, pot_ref, sems.at[0]),
        pltpu.make_async_copy(basis_hbm, basis_ref, sems.at[1]),
        pltpu.make_async_copy(ranks_hbm, ranks_ref, sems.at[2]),
    ]
    for copy in copies:
        copy.start()
    for copy in copies:
        copy.wait()
    pot = pot_ref[...].reshape(64, 512)
    basis = basis_ref[...].reshape(64, 512)
    both = jnp.concatenate([basis, basis], axis=0)
    full = lax.dot_general(pot, both, NT, preferred_element_type=F32)
    lane = lax.broadcasted_iota(jnp.int32, (16, 128), 1)
    here = (lane >> 6) == (p & 1)
    total = jnp.zeros((16, 128), F32)
    for j in range(4):
        keep = here & (((lane >> 4) & 3) == j) & ((lane & 15) < ranks_ref[j])
        total = total + jnp.where(keep, full[j * 16:(j + 1) * 16, :], 0.0)
    out_ref[...] = total.astype(BF16)


def join_kernel(mine_ref, theirs_ref, room_ref, out_ref):
    out_ref[0] = mine_ref[...] + theirs_ref[...]


def weights_kernel(near_half_ref, far_half_ref, couplings_ref, out_ref, sent_ref, gathered):
    p = lax.axis_index("prod")
    x = p >> 3
    y = (p >> 1) & 3
    for r in range(16):
        chip = (x ^ GRAY[r // 4]) * 4 + (y ^ GRAY[r % 4])
        piece = near_half_ref[r] if r < 8 else far_half_ref[r - 8]
        gathered[:, pl.ds(pl.multiple_of(chip * 128, 128), 128)] = piece
    weights = lax.dot_general(gathered[...], couplings_ref[...], NT, preferred_element_type=F32)
    out_ref[...] = weights
    sent_ref[...] = weights.astype(BF16)


def far_rows(piece, weights_ref, got_ref, row_ref):
    both = weights_ref[...] + got_ref[...].astype(F32)
    tall = jnp.concatenate([both] * 4, axis=0)
    row = lax.broadcasted_iota(jnp.int32, (64, 256), 0) >> 4
    col = lax.broadcasted_iota(jnp.int32, (64, 256), 1) >> 4
    spread = jnp.where(row + piece * 4 == col, tall, 0.0).astype(BF16)
    return jnp.dot(spread, row_ref[...], preferred_element_type=F32).reshape(4, 16, 512)


def select_kernel(own_ref, other_ref, group_ref, chip_ref, out_ref):
    _, a, core, first, second = place()
    for z in range(4):
        d = a ^ z
        slot = jnp.where(d == 0, 0, jnp.where(d == first, 1, jnp.where(d == second, 2, 3)))
        at = pl.multiple_of((slot & 1) * 4, 4)
        piece = jnp.where(slot < 2, own_ref[pl.ds(at, 4)], other_ref[pl.ds(at, 4)])
        group_ref[z * 4:(z + 1) * 4] = piece
        to_chip = (z < 2) == (core == 1) if False else ((z >> 1) ^ core) == 1

        @pl.when(to_chip)
        def _():
            chip_ref[(z & 1) * 4:(z & 1) * 4 + 4] = piece

        @pl.when(jnp.logical_not(to_chip))
        def _():
            out_ref[(z & 1) * 4:(z & 1) * 4 + 4] = piece


def near_kernel(keep, cols_ref, group_ref, chip_ref, outer_ref, near_ref, out_ref):
    p, a, core, first, second = place()
    base = p * 16
    for half in range(2):
        if keep:
            piece = a if half == 0 else a ^ second
        else:
            piece = a ^ first if half == 0 else a ^ 2
        for j in range(4):
            i = piece * 4 + j
            c = cols_ref[i] - base
            below = c < 0
            above = c >= 16
            halo = jnp.clip(jnp.where(below, c + 8, c - 16), 0, 7)
            from_chip = (below & (core == 1)) | (above & (core == 0))
            inside = jnp.logical_not(below | above)
            picked = jnp.where(from_chip, chip_ref[halo], outer_ref[halo])
            picked = jnp.where(inside, group_ref[jnp.clip(c, 0, 15)], picked)
            block = lax.dot_general(picked, near_ref[i], NT, preferred_element_type=F32)
            out_ref[half * 4 + j] = block.astype(out_ref.dtype)


def fold_kernel(kept_ref, got_ref, weights_ref, got_weights_ref, row_ref, out_ref):
    _, a, _, _, second = place()
    far = far_rows(a ^ second, weights_ref, got_weights_ref, row_ref)
    out_ref[...] = (kept_ref[4:8] + got_ref[4:8].astype(F32) + far).astype(BF16)


def own_kernel(kept_ref, got_ref, weights_ref, got_weights_ref, row_ref, injected_ref, out_ref):
    far = far_rows(lax.axis_index("pre"), weights_ref, got_weights_ref, row_ref)
    out_ref[...] = injected_ref[...] - (kept_ref[0:4] + got_ref[0:4].astype(F32) + far)


def final_kernel(own_ref, last_ref, inverse_ref, residual_ref, corrected_ref):
    for j in range(4):
        residual = own_ref[j] - last_ref[j].astype(F32)
        residual_ref[j] = residual
        corrected_ref[j] = lax.dot_general(
            residual.astype(BF16), inverse_ref[j], NT, preferred_element_type=F32
        )


VMEM = pl.BlockSpec(memory_space=pltpu.VMEM)
HBM = pl.BlockSpec(memory_space=pltpu.HBM)
SMEM = pl.BlockSpec(memory_space=pltpu.SMEM)


def call(kernel, out_shape, in_specs, scratch=(), flops=0, moved=0, limit=16 * 2**20, out_specs=None):
    many = isinstance(out_shape, (list, tuple))
    return pl.pallas_call(
        kernel,
        out_shape=out_shape,
        in_specs=in_specs,
        out_specs=out_specs or ([VMEM] * len(out_shape) if many else VMEM),
        scratch_shapes=list(scratch),
        compiler_params=pltpu.CompilerParams(vmem_limit_bytes=limit),
        cost_estimate=pl.CostEstimate(flops=flops, bytes_accessed=moved, transcendentals=0),
    )


def shape(dims, dtype):
    return jax.ShapeDtypeStruct(dims, dtype)


def compute(
    potentials,
    injected,
    near_blocks,
    near_cols,
    row_basis,
    col_basis,
    basis_ranks,
    couplings,
    inverses,
):
    first_z = send(potentials, Z_FIRST)
    coeffs, room = call(
        coeff_kernel, [pltpu.VMEM((16, 128), BF16), shape((20, 1024, 1024), BF16)], [HBM, HBM, HBM],
        scratch=[
            pltpu.VMEM((4, 16, 512), BF16), pltpu.VMEM((4, 16, 512), BF16), pltpu.SMEM((4,), jnp.int32),
            pltpu.SemaphoreType.DMA((3,)),
        ],
        moved=2**17, limit=63 * 2**20, out_specs=[VMEM, HBM],
    )(potentials, col_basis, basis_ranks)
    gathered = call(join_kernel, shape((1, 16, 128), BF16), [VMEM, VMEM, HBM], moved=2**25)(
        coeffs, send(coeffs, CORE_SWAP), room
    )
    for table in (Y_SWAPS[0], Y_SWAPS[1], X_SWAPS[0]):
        gathered = jnp.concatenate([gathered, send(gathered, table)], axis=0)
    others = send(gathered, X_SWAPS[1])
    own_pair = jnp.concatenate([potentials, first_z], axis=0)
    second_z = send(own_pair, Z_SECOND)
    group, to_chip, to_outer = call(
        select_kernel,
        [shape((16, 16, 512), BF16), shape((8, 16, 512), BF16), shape((8, 16, 512), BF16)],
        [VMEM, VMEM], moved=2**19,
    )(own_pair, second_z)
    outer = send(to_outer, OTHER_CHIP)
    chip = send(to_chip, CORE_SWAP)
    blocks = near_blocks.reshape(16, 512, 512)
    cols = near_cols.reshape(16)
    near_specs = [SMEM] + [VMEM] * 4
    sent = call(
        functools.partial(near_kernel, False), shape((8, 16, 512), BF16), near_specs,
        moved=2**22, flops=2**26,
    )(cols, group, chip, outer, blocks)
    got = send(sent, Z_FIRST)
    weights, sent_weights = call(
        weights_kernel, [shape((16, 256), F32), shape((16, 256), BF16)], [VMEM] * 3,
        scratch=[pltpu.VMEM((16, 2048), BF16)], moved=2**20, flops=2**24,
    )(gathered, others, couplings.reshape(256, 2048))
    got_weights = send(sent_weights, Z_FIRST)
    kept = call(
        functools.partial(near_kernel, True), shape((8, 16, 512), F32), near_specs,
        moved=2**22, flops=2**26,
    )(cols, group, chip, outer, blocks)
    rows = row_basis.reshape(256, 512)
    folded = call(fold_kernel, shape((4, 16, 512), BF16), [VMEM] * 5, moved=2**18)(
        kept, got, weights, got_weights, rows
    )
    last = send(folded, Z_SECOND)
    own = call(own_kernel, shape((4, 16, 512), F32), [VMEM] * 6, moved=2**18)(
        kept, got, weights, got_weights, rows, injected
    )
    return call(
        final_kernel, [shape((4, 16, 512), F32), shape((4, 16, 512), F32)], [VMEM] * 3,
        moved=2**21, flops=2**25,
    )(own, last, inverses)


def solution(mesh):
    return jax.shard_map(
        compute,
        mesh=mesh,
        in_specs=(
            P(("prod", "pre"), None, None),
            P(("prod", "pre"), None, None),
            P("prod", "pre", None, None),
            P("prod", "pre"),
            P("prod", None, None),
            P(("prod", "pre"), None, None),
            P(("prod", "pre")),
            P("prod", None, "pre"),
            P(("prod", "pre"), None, None),
        ),
        out_specs=(P(("prod", "pre"), None, None), P(("prod", "pre"), None, None)),
        check_vma=False,
    )
```
